32 devices in a mesh: sub: 16 (over z, y, core), coarse: 2 (over x).
Axes of the slice: x: 2, y: 2, z: 4, core: 2. Of those that a mesh axis runs over, the one named last changes fastest.
Arguments:
- loads: float32 [32, 32, 32, 128], P(('sub', 'coarse')), may hold values from -6 to 6
- diag_blocks: float32 [32, 32, 128, 128], P(('sub', 'coarse')), may hold values from -0.2 to 6.2
- off_blocks: float32 [32, 32, 2, 128, 128], P(('sub', 'coarse')), may hold values from -0.25 to 0.25
- off_index: int32 [32, 32, 2], P(('sub', 'coarse')), may hold values from 0 to 31, as said below
- couple_blocks: float32 [32, 2, 128, 128], P(('sub', 'coarse')), may hold values from -0.5 to 0.5
- basis: float32 [32, 128, 32, 128], P(('sub', 'coarse')), may hold values from -0.09375 to 0.09375
- coarse_blocks: float32 [32, 6, 128, 128], P(('sub', 'coarse')), may hold values from -0.21875 to 0.21875
- coarse_index: int32 [32, 6], P(('sub', 'coarse')), may hold values from 0 to 31, as said below
Outputs:
- solution: float32 [32, 32, 32, 128], P(('sub', 'coarse'))
- residual: float32 [32, 32, 32, 128], P(('sub', 'coarse'))
The draws below stay inside these ranges and needn't reach their ends.
Inputs may be any that keep to these rules, and one draw needn't show every extreme that they name: `off_index`: the 2 entries of a block row name different blocks of the same subdomain, none of them the row's own block. `coarse_index`: the 6 entries of a row name different subdomains, the first being the row's own subdomain g and the second g - 1 counted round.
All inputs are finite; a program needn't handle non-finite values.
Results may differ from the reference program's by a relative error of at most 0.0001.
Values sent between devices are 32-bit elements; how exact they have to be, the bound alone decides.
A program may use at most 128 MiB of HBM per device.

```python
import jax
import jax.numpy as jnp
from jax import lax

N_LOC = 4096
BS = 128
NB = 32
K = 128
COLS = 32
NOFF = 2
NCB = 6
ORDER = 5
ITERS = 2
SUBS = 32
N_SUB = 16
N_COARSE = 2


def draw_diag_blocks(key, part):
    key_diag, key_rest = jax.random.split(jax.random.fold_in(key, 11))
    values = jax.random.uniform(key_diag, (SUBS, NB, BS), jnp.float32, 3.0, 6.0)
    spread = 0.5 / BS ** 0.5
    rest = jax.random.normal(key_rest, (SUBS, NB, BS, BS), jnp.float32) * spread
    rest = jnp.clip(rest, -0.2, 0.2)
    return rest + values[..., None] * jnp.eye(BS, dtype=jnp.float32)


def draw_off_index(key, part):
    steps = jax.random.randint(jax.random.fold_in(key, 23), (SUBS, NB, NOFF), 1, NB // NOFF)
    offsets = jnp.cumsum(steps, axis=2)
    rows = jnp.arange(NB, dtype=jnp.int32)[None, :, None]
    return ((rows + offsets) % NB).astype(jnp.int32)


def draw_coarse_index(key, part):
    steps = jax.random.randint(jax.random.fold_in(key, 37), (SUBS, NCB - 2), 1, SUBS // NCB)
    rest = jnp.cumsum(steps, axis=1).astype(jnp.int32)
    own = jnp.zeros((SUBS, 1), jnp.int32)
    before = jnp.full((SUBS, 1), SUBS - 1, jnp.int32)
    offsets = jnp.concatenate([own, before, rest], axis=1)
    rows = jnp.arange(SUBS, dtype=jnp.int32)[:, None]
    return ((rows + offsets) % SUBS).astype(jnp.int32)


def shard_levels(stream_key, shape, cuts, low, largest):
    factor_of = 1.0
    for axis_at, parts in cuts:
        heights = jax.random.uniform(jax.random.fold_in(jax.random.fold_in(stream_key, 6), axis_at), (parts,), jnp.float32, low / len(cuts), largest / len(cuts))
        factor_of = factor_of * jnp.repeat(jnp.exp(heights), shape[axis_at] // parts).reshape((-1,) + (1,) * (len(shape) - 1 - axis_at))
    return factor_of


def scatter_about(key, shape, scale, bound, shards=(), kind=jnp.bfloat16):
    factor_of = shard_levels(key, shape, shards, -0.22, 0.18) if shards else 1.0
    drawn = jax.random.normal(key, shape, jnp.float32) * scale * factor_of
    return jnp.minimum(jnp.maximum(drawn, -bound), bound).astype(kind)


def setup_inputs(seed: int = 0) -> dict:
    streams_of = jax.random.split(jax.random.key(seed), 9)
    loads = scatter_about(streams_of[0], (SUBS, COLS, NB, BS), 1.0, 6.0, ((0, 32),), jnp.float32)
    diag_blocks = draw_diag_blocks(jax.random.fold_in(streams_of[8], 71), 0)
    off_blocks = scatter_about(streams_of[2], (SUBS, NB, NOFF, BS, BS), (4 * BS) ** -0.5, 0.25, ((0, 32),), jnp.float32)
    off_index = draw_off_index(jax.random.fold_in(streams_of[8], 71), 0)
    couple_blocks = scatter_about(streams_of[4], (SUBS, 2, BS, BS), BS ** -0.5, 0.5, ((0, 32),), jnp.float32)
    basis = scatter_about(streams_of[5], (SUBS, K, NB, BS), N_LOC ** -0.5, 0.09375, ((0, 32),), jnp.float32)
    coarse_blocks = scatter_about(streams_of[6], (SUBS, NCB, K, K), (NCB * K) ** -0.5, 0.21875, ((0, 32),), jnp.float32)
    coarse_index = draw_coarse_index(jax.random.fold_in(streams_of[8], 71), 0)
    return dict(loads=loads, diag_blocks=diag_blocks, off_blocks=off_blocks, off_index=off_index, couple_blocks=couple_blocks, basis=basis, coarse_blocks=coarse_blocks, coarse_index=coarse_index)


highest = lax.Precision.HIGHEST
theta_mid = 5.0
delta_half = 4.0


def from_left(value):
    shaped = value.reshape((N_SUB, N_COARSE) + value.shape[1:])
    shaped = jnp.concatenate([jnp.zeros_like(shaped[:1]), shaped[:-1]], axis=0)
    return shaped.reshape(value.shape)


def from_right(value):
    shaped = value.reshape((N_SUB, N_COARSE) + value.shape[1:])
    shaped = jnp.concatenate([shaped[1:], jnp.zeros_like(shaped[:1])], axis=0)
    return shaped.reshape(value.shape)


def own_rows(own, left_block, right_block, diag, offs, index, couple):
    result = jnp.einsum("cbk,bik->cbi", own, diag, precision=highest)
    picked = jnp.take(own, index, axis=1)
    result = result + jnp.einsum("cbjk,bjik->cbi", picked, offs, precision=highest)
    first = result[:, 0] + jnp.einsum("ck,ik->ci", left_block, couple[0], precision=highest)
    last = result[:, -1] + jnp.einsum("ck,ik->ci", right_block, couple[1], precision=highest)
    return result.at[:, 0].set(first).at[:, -1].set(last)


def padded_rows(padded, diag, offs, index, couple, left_diag, left_up, right_diag, right_low):
    middle = own_rows(padded[:, 1:-1], padded[:, 0], padded[:, -1], diag, offs, index, couple)
    top = jnp.einsum("ck,ik->ci", padded[:, 0], left_diag, precision=highest)
    top = top + jnp.einsum("ck,ik->ci", padded[:, 1], left_up, precision=highest)
    bottom = jnp.einsum("ck,ik->ci", padded[:, -1], right_diag, precision=highest)
    bottom = bottom + jnp.einsum("ck,ik->ci", padded[:, -2], right_low, precision=highest)
    return jnp.concatenate([top[:, None], middle, bottom[:, None]], axis=1)


def chebyshev(padded, diag, offs, index, couple, left_diag, left_up, right_diag, right_low):
    sigma = theta_mid / delta_half
    rho_now = 1.0 / sigma
    direction = padded / theta_mid
    smooth = jnp.zeros_like(padded)
    for step in range(ORDER):
        smooth = smooth + direction
        if step + 1 < ORDER:
            misfit = padded - padded_rows(smooth, diag, offs, index, couple, left_diag, left_up, right_diag, right_low)
            rho_next = 1.0 / (2.0 * sigma - rho_now)
            direction = rho_next * rho_now * direction + (2.0 * rho_next / delta_half) * misfit
            rho_now = rho_next
    return smooth


def reference(loads, diag_blocks, off_blocks, off_index, couple_blocks, basis, coarse_blocks, coarse_index):
    left_diag = from_left(diag_blocks[:, -1])
    left_up = from_left(couple_blocks[:, 1])
    right_diag = from_right(diag_blocks[:, 0])
    right_low = from_right(couple_blocks[:, 0])
    solution = jnp.zeros_like(loads)
    resid = loads
    for step in range(ITERS):
        padded = jnp.concatenate([from_left(resid[:, :, -1])[:, :, None], resid, from_right(resid[:, :, 0])[:, :, None]], axis=2)
        smooth = jax.vmap(chebyshev)(padded, diag_blocks, off_blocks, off_index, couple_blocks, left_diag, left_up, right_diag, right_low)
        coeffs = jnp.einsum("scbi,skbi->sck", resid, basis, precision=highest)
        picked = coeffs[coarse_index]
        coarse_sol = jnp.einsum("sjck,sjik->sci", picked, coarse_blocks, precision=highest)
        edge = smooth[:, :, 1:-1] + jnp.einsum("sck,skbi->scbi", coarse_sol, basis, precision=highest)
        first = edge[:, :, 0] + from_left(smooth[:, :, -1])
        last = edge[:, :, -1] + from_right(smooth[:, :, 0])
        change = edge.at[:, :, 0].set(first).at[:, :, -1].set(last)
        solution = solution + change
        applied = jax.vmap(own_rows)(change, from_left(change[:, :, -1]), from_right(change[:, :, 0]), diag_blocks, off_blocks, off_index, couple_blocks)
        resid = resid - applied
    return solution, resid
```

```python
import functools

import jax
import jax.numpy as jnp
from jax import lax
from jax.experimental import pallas as pl
from jax.experimental.pallas import tpu as pltpu
from jax.sharding import PartitionSpec as P

ORDER = 5
ITERS = 2
THETA = 5.0
DELTA = 4.0
F32 = jnp.float32
BF16 = jnp.bfloat16
MESH = pl.DeviceIdType.MESH


def cheb_coefs():
    sigma = THETA / DELTA
    rho = 1.0 / sigma
    out = []
    for _ in range(ORDER - 1):
        nxt = 1.0 / (2.0 * sigma - rho)
        out.append((nxt * rho, 2.0 * nxt / DELTA))
        rho = nxt
    return out


def halves(v):
    hi = v.astype(BF16)
    lo = (v - hi.astype(F32)).astype(BF16)
    return hi, lo


def dot_nt(x, w):
    return lax.dot_general(x, w, (((1,), (1,)), ((), ())), preferred_element_type=F32)


def dot_nn(x, w):
    return lax.dot_general(x, w, (((1,), (0,)), ((), ())), preferred_element_type=F32)


def kernel(
    ns, nc, nb, cols, bs, ncb,
    loads, diag, offs, oidx, couple, basis, cblk, cidx,
    sol, res,
    f_loads, f_diag, f_offs, f_couple, f_basis, f_cblk,
    w, wc, wt, bw, cw,
    r, d, z, ua, ub, ur,
    gath0, gath1, op_in, r_in, e_in, e_out,
    lsem, op_s, op_r, rh_s, rh_r, e_s, e_r, g1_s, g1_r, g2_s, g2_r, g3_s, g3_r,
):
    me_s = lax.axis_index("sub")
    me_x = lax.axis_index("coarse")
    core = lax.rem(me_s, 2)
    h = me_s // 2
    half = ns // 2
    partner = me_s + 1 - 2 * core
    has_l = me_s > 0
    has_r = me_s < ns - 1
    nb2 = nb // 2
    left, right = nb, nb + 1

    ld = [
        pltpu.make_async_copy(loads, f_loads, lsem.at[0]),
        pltpu.make_async_copy(basis, f_basis, lsem.at[1]),
        pltpu.make_async_copy(couple, f_couple, lsem.at[2]),
        pltpu.make_async_copy(diag, f_diag, lsem.at[3]),
        pltpu.make_async_copy(offs, f_offs, lsem.at[4]),
        pltpu.make_async_copy(cblk, f_cblk, lsem.at[5]),
    ]
    for c in ld:
        c.start()

    def remote(src, dst, ss, rs, s, x):
        return pltpu.make_async_remote_copy(
            src_ref=src, dst_ref=dst, send_sem=ss, recv_sem=rs,
            device_id={"sub": s, "coarse": x}, device_id_type=MESH,
        )

    barrier = pltpu.get_barrier_semaphore()

    def greet(s, x):
        pl.semaphore_signal(
            barrier, inc=1, device_id={"sub": s, "coarse": x}, device_id_type=MESH
        )

    for k in range(1, half):
        greet(core + 2 * lax.rem(h + k, half), me_x)
    for k in range(1, nc):
        greet(me_s, lax.rem(me_x + k, nc))

    @pl.when(has_l)
    def _():
        greet(me_s - 1, me_x)

    @pl.when(has_r)
    def _():
        greet(me_s + 1, me_x)

    def put(ref, b, v):
        hi, lo = halves(v)
        ref[b, 0:cols, :] = hi
        ref[b, cols : 2 * cols, :] = lo

    def fold(o):
        return (o[:cols, :bs] + o[:cols, bs:]) + (o[cols:, :bs] + o[cols:, bs:])

    ld[0].wait()

    def init_r(b, carry):
        v = f_loads[pl.ds(b, cols, stride=nb), :]
        r[b] = v
        put(ur, b, v)
        return carry

    lax.fori_loop(0, nb, init_r, 0)
    ld[1].wait()

    def init_bw(t, carry):
        for p in range(2):
            v = f_basis[pl.ds(2 * t + p, bs, stride=nb), :]
            hi, lo = halves(v)
            bw[t, 0:bs, p * bs : (p + 1) * bs] = hi
            bw[t, bs : 2 * bs, p * bs : (p + 1) * bs] = lo
        return carry

    lax.fori_loop(0, nb2, init_bw, 0)

    pl.semaphore_wait(barrier, half - 1 + nc - 1 + has_l.astype(jnp.int32) + has_r.astype(jnp.int32))

    def op_copies(to_left):
        b = 0 if to_left else nb - 1
        side = 1 if to_left else 0
        s = me_s - 1 if to_left else me_s + 1
        return [
            remote(f_diag.at[b], op_in.at[side, 0], op_s.at[side, 0], op_r.at[side, 0], s, me_x),
            remote(
                f_couple.at[0 if to_left else 1], op_in.at[side, 1],
                op_s.at[side, 1], op_r.at[side, 1], s, me_x,
            ),
        ]

    def r_copy(it, to_left):
        b = 0 if to_left else nb - 1
        side = 1 if to_left else 0
        s = me_s - 1 if to_left else me_s + 1
        return [remote(r.at[b], r_in.at[it, side], rh_s.at[it, side], rh_r.at[it, side], s, me_x)]

    def e_copy(it, to_left):
        side = 1 if to_left else 0
        s = me_s - 1 if to_left else me_s + 1
        return [
            remote(
                e_out.at[it, side], e_in.at[it, side], e_s.at[it, side], e_r.at[it, side], s, me_x
            )
        ]

    def start_both(make):
        @pl.when(has_l)
        def _():
            for c in make(True):
                c.start()

        @pl.when(has_r)
        def _():
            for c in make(False):
                c.start()

    def wait_both(make):
        @pl.when(has_l)
        def _():
            for c in make(True):
                c.wait_send()
            for c in make(False):
                c.wait_recv()

        @pl.when(has_r)
        def _():
            for c in make(False):
                c.wait_send()
            for c in make(True):
                c.wait_recv()

    for side, has in ((0, has_l), (1, has_r)):

        @pl.when(jnp.logical_not(has))
        def _():
            op_in[side] = jnp.zeros_like(op_in[side])
            for it in range(ITERS):
                r_in[it, side] = jnp.zeros_like(r_in[it, side])
                e_in[it, side] = jnp.zeros_like(e_in[it, side])

    own = me_x * half + h
    gath = (gath0, gath1)

    def g1(it):
        return [
            remote(
                gath[it].at[core, own], gath[it].at[core, own],
                g1_s.at[it, k - 1], g1_r.at[it, k - 1],
                core + 2 * lax.rem(h + k, half), me_x,
            )
            for k in range(1, half)
        ]

    def g2(it):
        span = pl.ds(me_x * half, half)
        return [
            remote(
                gath[it].at[core, span], gath[it].at[core, span],
                g2_s.at[it, k - 1], g2_r.at[it, k - 1],
                me_s, lax.rem(me_x + k, nc),
            )
            for k in range(1, nc)
        ]

    def g3(it):
        return [
            remote(
                gath[it].at[core], gath[it].at[core], g3_s.at[it], g3_r.at[it], partner, me_x
            )
        ]

    def start(copies):
        for c in copies:
            c.start()

    def wait(copies):
        for c in copies:
            c.wait()

    def coeffs(it):
        def body(q, acc):
            for p in range(4):
                t = 4 * q + p
                x = jnp.concatenate([ur[2 * t], ur[2 * t + 1]], axis=1)
                acc = acc + dot_nt(x, bw[t])
            return acc

        acc = lax.fori_loop(0, nb2 // 4, body, jnp.zeros((2 * cols, 2 * bs), F32))
        gath[it][core, own] = fold(acc)

    def row(u, b):
        x = jnp.concatenate([u[b], u[oidx[b, 0]], u[oidx[b, 1]]], axis=1)
        return fold(dot_nt(x, w[b]))

    GROUP = 6

    def middle(u, emit):
        def body(q, carry):
            rows = [1 + q * GROUP + p for p in range(GROUP)]
            ys = [row(u, b) for b in rows]
            emit(rows, ys)
            return carry

        lax.fori_loop(0, (nb - 2) // GROUP, body, 0)

    def first_last(u):
        y0 = row(u, 0) + fold(dot_nt(u[left], wc[0]))
        y1 = row(u, nb - 1) + fold(dot_nt(u[right], wc[1]))
        return y0, y1

    def outer(u):
        yl = fold(dot_nt(jnp.concatenate([u[left], u[0]], axis=1), wt[0]))
        yr = fold(dot_nt(jnp.concatenate([u[right], u[nb - 1]], axis=1), wt[1]))
        return yl, yr

    coefs = cheb_coefs()

    def emit_step(k, unew):
        ca, cc = coefs[k]

        def emit(rows, ys):
            out = []
            for b, y in zip(rows, ys):
                rv = r[b]
                if k == 0:
                    dv = rv * (1.0 / THETA)
                    zv = dv
                    y = y * (1.0 / THETA)
                else:
                    dv = d[b]
                    zv = z[b]
                dv = ca * dv + cc * (rv - y)
                out.append((dv, zv + dv))
            for b, (dv, zv) in zip(rows, out):
                if k + 2 < ORDER:
                    d[b] = dv
                    put(unew, b, zv)
                z[b] = zv

        return emit

    def ends_step(k, u, unew):
        yl, yr = outer(u)
        y0, y1 = first_last(u)
        emit_step(k, unew)([0, nb - 1, left, right], [y0, y1, yl, yr])

    def iteration(it):
        last = it + 1 == ITERS
        middle(ur, emit_step(0, ua))
        wait_both(functools.partial(r_copy, it))
        for side, b in ((0, left), (1, right)):
            v = r_in[it, side]
            r[b] = v
            put(ur, b, v)
        ends_step(0, ur, ua)
        wait(g1(it))
        start(g2(it))
        middle(ua, emit_step(1, ub))
        ends_step(1, ua, ub)
        middle(ub, emit_step(2, ua))
        ends_step(2, ub, ua)
        wait(g2(it))
        start(g3(it))
        ends_step(3, ua, ub)
        middle(ua, emit_step(3, ub))
        wait(g3(it))

        xs = []
        for j in range(ncb):
            g = cidx[j]
            s = g // nc
            x = lax.rem(g, nc)
            hi, lo = halves(gath[it][lax.rem(s, 2), x * half + s // 2])
            xs.append(jnp.concatenate([hi, lo], axis=0))
        csol = fold(dot_nt(jnp.concatenate(xs, axis=1), cw[...]))
        hi, lo = halves(csol)
        cx = jnp.concatenate([hi, lo], axis=0)
        cx = jnp.concatenate([cx, cx], axis=1)

        def spread(t):
            o = dot_nn(cx, bw[t])
            o = o[:cols] + o[cols:]
            return o[:, :bs], o[:, bs:]

        def keep(b, v):
            sol[b] = v if it == 0 else sol[b] + v
            put(ub, b, v)

        a0, a1 = spread(0)
        b0, b1 = spread(nb2 - 1)
        edge_l = z[0] + a0
        edge_r = z[nb - 1] + b1
        e_out[it, 1, 0] = z[left]
        e_out[it, 1, 1] = edge_l
        e_out[it, 0, 0] = z[right]
        e_out[it, 0, 1] = edge_r
        start_both(functools.partial(e_copy, it))
        keep(1, z[1] + a1)
        keep(nb - 2, z[nb - 2] + b0)

        def spread_body(q, carry):
            for p in range(2):
                t = 1 + 2 * q + p
                v0, v1 = spread(t)
                keep(2 * t, z[2 * t] + v0)
                keep(2 * t + 1, z[2 * t + 1] + v1)
            return carry

        lax.fori_loop(0, (nb2 - 2) // 2, spread_body, 0)
        wait_both(functools.partial(e_copy, it))
        keep(0, edge_l + e_in[it, 0, 0])
        keep(nb - 1, edge_r + e_in[it, 1, 0])
        put(ub, left, e_in[it, 0, 1] + z[left])
        put(ub, right, e_in[it, 1, 1] + z[right])

        def emit_res(rows, ys):
            vals = [r[b] - y for b, y in zip(rows, ys)]
            for b, v in zip(rows, vals):
                if last:
                    res[b] = v
                else:
                    r[b] = v
                    put(ur, b, v)

        emit_res([0, nb - 1], list(first_last(ub)))
        if not last:
            start_both(functools.partial(r_copy, it + 1))
        middle(ub, emit_res)
        if not last:
            coeffs(it + 1)
            start(g1(it + 1))

    start_both(functools.partial(r_copy, 0))
    coeffs(0)
    start(g1(0))
    ld[2].wait()
    ld[3].wait()
    start_both(op_copies)
    ld[4].wait()

    def init_w(b, carry):
        for j, v in enumerate((f_diag[b], f_offs[b, 0], f_offs[b, 1])):
            hi, lo = halves(v)
            w[b, 0:bs, j * bs : (j + 1) * bs] = hi
            w[b, bs : 2 * bs, j * bs : (j + 1) * bs] = lo
        return carry

    lax.fori_loop(0, nb, init_w, 0)
    for j in range(2):
        hi, lo = halves(f_couple[j])
        wc[j, 0:bs, :] = hi
        wc[j, bs : 2 * bs, :] = lo
    ld[5].wait()
    for j in range(ncb):
        hi, lo = halves(f_cblk[j])
        cw[0:bs, j * bs : (j + 1) * bs] = hi
        cw[bs : 2 * bs, j * bs : (j + 1) * bs] = lo
    wait_both(op_copies)
    for side in range(2):
        for j in range(2):
            hi, lo = halves(op_in[side, j])
            wt[side, 0:bs, j * bs : (j + 1) * bs] = hi
            wt[side, bs : 2 * bs, j * bs : (j + 1) * bs] = lo

    for it in range(ITERS):
        iteration(it)


def per_device(ns, nc, loads, diag, offs, oidx, couple, basis, cblk, cidx):
    _, cols, nb, bs = loads.shape
    k = basis.shape[1]
    ncb = cblk.shape[1]
    half = ns // 2
    anyspace = pl.BlockSpec(memory_space=pl.ANY)
    smem = pl.BlockSpec(memory_space=pltpu.SMEM)
    vmem = pl.BlockSpec(memory_space=pltpu.VMEM)
    field = (nb + 2, cols, bs)
    ufield = (nb + 2, 2 * cols, bs)
    dma = pltpu.SemaphoreType.DMA
    out = jax.ShapeDtypeStruct((nb, cols, bs), F32)
    sol, res = pl.pallas_call(
        functools.partial(kernel, ns, nc, nb, cols, bs, ncb),
        out_shape=(out, out),
        in_specs=[anyspace, anyspace, anyspace, smem, anyspace, anyspace, anyspace, smem],
        out_specs=(vmem, vmem),
        scratch_shapes=[
            pltpu.VMEM((cols * nb, bs), F32),
            pltpu.VMEM((nb, bs, bs), F32),
            pltpu.VMEM((nb, 2, bs, bs), F32),
            pltpu.VMEM((2, bs, bs), F32),
            pltpu.VMEM((k * nb, bs), F32),
            pltpu.VMEM((ncb, bs, bs), F32),
            pltpu.VMEM((nb, 2 * bs, 3 * bs), BF16),
            pltpu.VMEM((2, 2 * bs, bs), BF16),
            pltpu.VMEM((2, 2 * bs, 2 * bs), BF16),
            pltpu.VMEM((nb // 2, 2 * bs, 2 * bs), BF16),
            pltpu.VMEM((2 * bs, ncb * bs), BF16),
            pltpu.VMEM(field, F32),
            pltpu.VMEM(field, F32),
            pltpu.VMEM(field, F32),
            pltpu.VMEM(ufield, BF16),
            pltpu.VMEM(ufield, BF16),
            pltpu.VMEM(ufield, BF16),
            pltpu.VMEM((2, nc * half, cols, bs), F32),
            pltpu.VMEM((2, nc * half, cols, bs), F32),
            pltpu.VMEM((2, 2, bs, bs), F32),
            pltpu.VMEM((ITERS, 2, cols, bs), F32),
            pltpu.VMEM((ITERS, 2, 2, cols, bs), F32),
            pltpu.VMEM((ITERS, 2, 2, cols, bs), F32),
            dma((6,)),
            dma((2, 2)),
            dma((2, 2)),
            dma((ITERS, 2)),
            dma((ITERS, 2)),
            dma((ITERS, 2)),
            dma((ITERS, 2)),
            dma((ITERS, half - 1)),
            dma((ITERS, half - 1)),
            dma((ITERS, nc - 1)),
            dma((ITERS, nc - 1)),
            dma((ITERS,)),
            dma((ITERS,)),
        ],
        compiler_params=pltpu.CompilerParams(
            collective_id=0, has_side_effects=True, vmem_limit_bytes=56 * 1024 * 1024
        ),
    )(
        loads.reshape(cols * nb, bs), diag[0], offs[0], oidx[0], couple[0],
        basis.reshape(k * nb, bs), cblk[0], cidx[0],
    )
    return sol.transpose(1, 0, 2)[None], res.transpose(1, 0, 2)[None]


def solution(mesh):
    lead = ("sub", "coarse")
    in_specs = (
        P(lead, None, None, None),
        P(lead, None, None, None),
        P(lead, None, None, None, None),
        P(lead, None, None),
        P(lead, None, None, None),
        P(lead, None, None, None),
        P(lead, None, None, None),
        P(lead, None),
    )
    out_specs = (P(lead, None, None, None), P(lead, None, None, None))
    return jax.shard_map(
        functools.partial(per_device, mesh.shape["sub"], mesh.shape["coarse"]),
        mesh=mesh, in_specs=in_specs, out_specs=out_specs, check_vma=False,
    )
```

```python
import functools

import jax
import jax.numpy as jnp
from jax import lax
from jax.experimental import pallas as pl
from jax.experimental.pallas import tpu as pltpu
from jax.sharding import PartitionSpec as P

ORDER = 5
ITERS = 2
THETA = 5.0
DELTA = 4.0
F32 = jnp.float32
BF16 = jnp.bfloat16
MESH = pl.DeviceIdType.MESH


def cheb_coefs():
    sigma = THETA / DELTA
    rho = 1.0 / sigma
    out = []
    for _ in range(ORDER - 1):
        nxt = 1.0 / (2.0 * sigma - rho)
        out.append((nxt * rho, 2.0 * nxt / DELTA))
        rho = nxt
    return out


def halves(v):
    hi = v.astype(BF16)
    lo = (v - hi.astype(F32)).astype(BF16)
    return hi, lo


def dot_nt(x, w):
    return lax.dot_general(x, w, (((1,), (1,)), ((), ())), preferred_element_type=F32)


def dot_nn(x, w):
    return lax.dot_general(x, w, (((1,), (0,)), ((), ())), preferred_element_type=F32)


def kernel(
    ns, nc, nb, cols, bs, ncb,
    loads, diag, offs, oidx, couple, basis, cblk, cidx,
    sol, res,
    f_loads, f_diag, f_offs, f_couple, f_basis, f_cblk,
    w, wc, wt, bw, cw,
    r, d, z, ua, ub, ur,
    gath0, gath1, op_in, r_in, e_in, e_out,
    lsem, op_s, op_r, rh_s, rh_r, e_s, e_r, g1_s, g1_r, g2_s, g2_r, g3_s, g3_r,
):
    me_s = lax.axis_index("sub")
    me_x = lax.axis_index("coarse")
    core = lax.rem(me_s, 2)
    h = me_s // 2
    half = ns // 2
    partner = me_s + 1 - 2 * core
    has_l = me_s > 0
    has_r = me_s < ns - 1
    nb2 = nb // 2
    left, right = nb, nb + 1

    ld = [
        pltpu.make_async_copy(loads, f_loads, lsem.at[0]),
        pltpu.make_async_copy(basis, f_basis, lsem.at[1]),
        pltpu.make_async_copy(couple, f_couple, lsem.at[2]),
        pltpu.make_async_copy(diag, f_diag, lsem.at[3]),
        pltpu.make_async_copy(offs, f_offs, lsem.at[4]),
        pltpu.make_async_copy(cblk, f_cblk, lsem.at[5]),
    ]
    for c in ld:
        c.start()

    def remote(src, dst, ss, rs, s, x):
        return pltpu.make_async_remote_copy(
            src_ref=src, dst_ref=dst, send_sem=ss, recv_sem=rs,
            device_id={"sub": s, "coarse": x}, device_id_type=MESH,
        )

    barrier = pltpu.get_barrier_semaphore()

    def greet(s, x):
        pl.semaphore_signal(
            barrier, inc=1, device_id={"sub": s, "coarse": x}, device_id_type=MESH
        )

    for k in range(1, half):
        greet(core + 2 * lax.rem(h + k, half), me_x)
    for k in range(1, nc):
        greet(me_s, lax.rem(me_x + k, nc))

    @pl.when(has_l)
    def _():
        greet(me_s - 1, me_x)

    @pl.when(has_r)
    def _():
        greet(me_s + 1, me_x)

    def put(ref, b, v):
        hi, lo = halves(v)
        ref[b, 0:cols, :] = hi
        ref[b, cols : 2 * cols, :] = lo

    def fold(o):
        return (o[:cols, :bs] + o[:cols, bs:]) + (o[cols:, :bs] + o[cols:, bs:])

    ld[0].wait()

    def init_r(b, carry):
        v = f_loads[pl.ds(b, cols, stride=nb), :]
        r[b] = v
        put(ur, b, v)
        return carry

    lax.fori_loop(0, nb, init_r, 0)
    ld[1].wait()

    def init_bw(t, carry):
        for p in range(2):
            v = f_basis[pl.ds(2 * t + p, bs, stride=nb), :]
            hi, lo = halves(v)
            bw[t, 0:bs, p * bs : (p + 1) * bs] = hi
            bw[t, bs : 2 * bs, p * bs : (p + 1) * bs] = lo
        return carry

    lax.fori_loop(0, nb2, init_bw, 0)

    pl.semaphore_wait(barrier, half - 1 + nc - 1 + has_l.astype(jnp.int32) + has_r.astype(jnp.int32))

    def op_copies(to_left):
        b = 0 if to_left else nb - 1
        side = 1 if to_left else 0
        s = me_s - 1 if to_left else me_s + 1
        return [
            remote(f_diag.at[b], op_in.at[side, 0], op_s.at[side, 0], op_r.at[side, 0], s, me_x),
            remote(
                f_couple.at[0 if to_left else 1], op_in.at[side, 1],
                op_s.at[side, 1], op_r.at[side, 1], s, me_x,
            ),
        ]

    def r_copy(it, to_left):
        b = 0 if to_left else nb - 1
        side = 1 if to_left else 0
        s = me_s - 1 if to_left else me_s + 1
        return [remote(r.at[b], r_in.at[it, side], rh_s.at[it, side], rh_r.at[it, side], s, me_x)]

    def e_copy(it, to_left):
        side = 1 if to_left else 0
        s = me_s - 1 if to_left else me_s + 1
        return [
            remote(
                e_out.at[it, side], e_in.at[it, side], e_s.at[it, side], e_r.at[it, side], s, me_x
            )
        ]

    def start_both(make):
        @pl.when(has_l)
        def _():
            for c in make(True):
                c.start()

        @pl.when(has_r)
        def _():
            for c in make(False):
                c.start()

    def wait_both(make):
        @pl.when(has_l)
        def _():
            for c in make(True):
                c.wait_send()
            for c in make(False):
                c.wait_recv()

        @pl.when(has_r)
        def _():
            for c in make(False):
                c.wait_send()
            for c in make(True):
                c.wait_recv()

    for side, has in ((0, has_l), (1, has_r)):

        @pl.when(jnp.logical_not(has))
        def _():
            op_in[side] = jnp.zeros_like(op_in[side])
            for it in range(ITERS):
                r_in[it, side] = jnp.zeros_like(r_in[it, side])
                e_in[it, side] = jnp.zeros_like(e_in[it, side])

    own = me_x * half + h
    gath = (gath0, gath1)

    def g1(it):
        return [
            remote(
                gath[it].at[core, own], gath[it].at[core, own],
                g1_s.at[it, k - 1], g1_r.at[it, k - 1],
                core + 2 * lax.rem(h + k, half), me_x,
            )
            for k in range(1, half)
        ]

    def g2(it):
        span = pl.ds(me_x * half, half)
        return [
            remote(
                gath[it].at[core, span], gath[it].at[core, span],
                g2_s.at[it, k - 1], g2_r.at[it, k - 1],
                me_s, lax.rem(me_x + k, nc),
            )
            for k in range(1, nc)
        ]

    def g3(it):
        return [
            remote(
                gath[it].at[core], gath[it].at[core], g3_s.at[it], g3_r.at[it], partner, me_x
            )
        ]

    def start(copies):
        for c in copies:
            c.start()

    def wait(copies):
        for c in copies:
            c.wait()

    def coeffs(it):
        def body(q, acc):
            for p in range(4):
                t = 4 * q + p
                x = jnp.concatenate([ur[2 * t], ur[2 * t + 1]], axis=1)
                acc = acc + dot_nt(x, bw[t])
            return acc

        acc = lax.fori_loop(0, nb2 // 4, body, jnp.zeros((2 * cols, 2 * bs), F32))
        gath[it][core, own] = fold(acc)

    def row(u, b):
        x = jnp.concatenate([u[b], u[oidx[0, b]], u[oidx[1, b]]], axis=1)
        return fold(dot_nn(x, w[b]))

    GROUP = 15
    BATCH = 5

    def middle(u, emit):
        def body(q, carry):
            for first in range(0, GROUP, BATCH):
                rows = [1 + q * GROUP + first + p for p in range(BATCH)]
                emit(rows, [row(u, b) for b in rows])
            return carry

        if GROUP == nb - 2:
            body(0, 0)
        else:
            lax.fori_loop(0, (nb - 2) // GROUP, body, 0)

    def first_last(u):
        y0 = row(u, 0) + fold(dot_nn(u[left], wc[0]))
        y1 = row(u, nb - 1) + fold(dot_nn(u[right], wc[1]))
        return y0, y1

    def outer(u):
        yl = fold(dot_nn(jnp.concatenate([u[left], u[0]], axis=1), wt[0]))
        yr = fold(dot_nn(jnp.concatenate([u[right], u[nb - 1]], axis=1), wt[1]))
        return yl, yr

    coefs = cheb_coefs()

    def emit_step(k, unew):
        ca, cc = coefs[k]

        def emit(rows, ys):
            out = []
            for b, y in zip(rows, ys):
                rv = r[b]
                if k == 0:
                    dv = rv * (1.0 / THETA)
                    zv = dv
                    y = y * (1.0 / THETA)
                else:
                    dv = d[b]
                    zv = z[b]
                dv = ca * dv + cc * (rv - y)
                out.append((dv, zv + dv))
            for b, (dv, zv) in zip(rows, out):
                if k + 2 < ORDER:
                    d[b] = dv
                    put(unew, b, zv)
                z[b] = zv

        return emit

    def ends_step(k, u, unew):
        yl, yr = outer(u)
        y0, y1 = first_last(u)
        emit_step(k, unew)([0, nb - 1, left, right], [y0, y1, yl, yr])

    def iteration(it):
        last = it + 1 == ITERS
        middle(ur, emit_step(0, ua))
        wait_both(functools.partial(r_copy, it))
        for side, b in ((0, left), (1, right)):
            v = r_in[it, side]
            r[b] = v
            put(ur, b, v)
        ends_step(0, ur, ua)
        wait(g1(it))
        start(g2(it))
        middle(ua, emit_step(1, ub))
        ends_step(1, ua, ub)
        middle(ub, emit_step(2, ua))
        ends_step(2, ub, ua)
        wait(g2(it))
        start(g3(it))
        ends_step(3, ua, ub)
        middle(ua, emit_step(3, ub))
        wait(g3(it))

        xs = []
        for j in range(ncb):
            g = cidx[j]
            s = g // nc
            x = lax.rem(g, nc)
            hi, lo = halves(gath[it][lax.rem(s, 2), x * half + s // 2])
            xs.append(jnp.concatenate([hi, lo], axis=0))
        csol = fold(dot_nt(jnp.concatenate(xs, axis=1), cw[...]))
        hi, lo = halves(csol)
        cx = jnp.concatenate([hi, lo], axis=0)
        cx = jnp.concatenate([cx, cx], axis=1)

        def spread(t):
            o = dot_nn(cx, bw[t])
            o = o[:cols] + o[cols:]
            return o[:, :bs], o[:, bs:]

        def keep(b, v):
            sol[b] = v if it == 0 else sol[b] + v
            put(ub, b, v)

        a0, a1 = spread(0)
        b0, b1 = spread(nb2 - 1)
        edge_l = z[0] + a0
        edge_r = z[nb - 1] + b1
        e_out[it, 1, 0] = z[left]
        e_out[it, 1, 1] = edge_l
        e_out[it, 0, 0] = z[right]
        e_out[it, 0, 1] = edge_r
        start_both(functools.partial(e_copy, it))
        keep(1, z[1] + a1)
        keep(nb - 2, z[nb - 2] + b0)

        def spread_body(q, carry):
            for p in range(2):
                t = 1 + 2 * q + p
                v0, v1 = spread(t)
                keep(2 * t, z[2 * t] + v0)
                keep(2 * t + 1, z[2 * t + 1] + v1)
            return carry

        lax.fori_loop(0, (nb2 - 2) // 2, spread_body, 0)
        wait_both(functools.partial(e_copy, it))
        keep(0, edge_l + e_in[it, 0, 0])
        keep(nb - 1, edge_r + e_in[it, 1, 0])
        put(ub, left, e_in[it, 0, 1] + z[left])
        put(ub, right, e_in[it, 1, 1] + z[right])

        def emit_res(rows, ys):
            vals = [r[b] - y for b, y in zip(rows, ys)]
            for b, v in zip(rows, vals):
                if last:
                    res[b] = v
                else:
                    r[b] = v
                    put(ur, b, v)

        emit_res([0, nb - 1], list(first_last(ub)))
        if not last:
            start_both(functools.partial(r_copy, it + 1))
        middle(ub, emit_res)
        if not last:
            coeffs(it + 1)
            start(g1(it + 1))

    start_both(functools.partial(r_copy, 0))
    coeffs(0)
    start(g1(0))
    ld[2].wait()
    ld[3].wait()
    start_both(op_copies)
    ld[4].wait()

    def init_w(b, carry):
        for j, v in enumerate((f_diag[b], f_offs[b, 0], f_offs[b, 1])):
            hi, lo = halves(v.T)
            w[b, j * bs : (j + 1) * bs, 0:bs] = hi
            w[b, j * bs : (j + 1) * bs, bs : 2 * bs] = lo
        return carry

    lax.fori_loop(0, nb, init_w, 0)
    for j in range(2):
        hi, lo = halves(f_couple[j].T)
        wc[j, :, 0:bs] = hi
        wc[j, :, bs : 2 * bs] = lo
    ld[5].wait()
    for j in range(ncb):
        hi, lo = halves(f_cblk[j])
        cw[0:bs, j * bs : (j + 1) * bs] = hi
        cw[bs : 2 * bs, j * bs : (j + 1) * bs] = lo
    wait_both(op_copies)
    for side in range(2):
        for j in range(2):
            hi, lo = halves(op_in[side, j].T)
            wt[side, j * bs : (j + 1) * bs, 0:bs] = hi
            wt[side, j * bs : (j + 1) * bs, bs : 2 * bs] = lo

    for it in range(ITERS):
        iteration(it)


def per_device(ns, nc, loads, diag, offs, oidx, couple, basis, cblk, cidx):
    _, cols, nb, bs = loads.shape
    k = basis.shape[1]
    ncb = cblk.shape[1]
    half = ns // 2
    anyspace = pl.BlockSpec(memory_space=pl.ANY)
    smem = pl.BlockSpec(memory_space=pltpu.SMEM)
    vmem = pl.BlockSpec(memory_space=pltpu.VMEM)
    field = (nb + 2, cols, bs)
    ufield = (nb + 2, 2 * cols, bs)
    dma = pltpu.SemaphoreType.DMA
    out = jax.ShapeDtypeStruct((nb, cols, bs), F32)
    sol, res = pl.pallas_call(
        functools.partial(kernel, ns, nc, nb, cols, bs, ncb),
        out_shape=(out, out),
        in_specs=[anyspace, anyspace, anyspace, smem, anyspace, anyspace, anyspace, smem],
        out_specs=(vmem, vmem),
        scratch_shapes=[
            pltpu.VMEM((cols * nb, bs), F32),
            pltpu.VMEM((nb, bs, bs), F32),
            pltpu.VMEM((nb, 2, bs, bs), F32),
            pltpu.VMEM((2, bs, bs), F32),
            pltpu.VMEM((k * nb, bs), F32),
            pltpu.VMEM((ncb, bs, bs), F32),
            pltpu.VMEM((nb, 3 * bs, 2 * bs), BF16),
            pltpu.VMEM((2, bs, 2 * bs), BF16),
            pltpu.VMEM((2, 2 * bs, 2 * bs), BF16),
            pltpu.VMEM((nb // 2, 2 * bs, 2 * bs), BF16),
            pltpu.VMEM((2 * bs, ncb * bs), BF16),
            pltpu.VMEM(field, F32),
            pltpu.VMEM(field, F32),
            pltpu.VMEM(field, F32),
            pltpu.VMEM(ufield, BF16),
            pltpu.VMEM(ufield, BF16),
            pltpu.VMEM(ufield, BF16),
            pltpu.VMEM((2, nc * half, cols, bs), F32),
            pltpu.VMEM((2, nc * half, cols, bs), F32),
            pltpu.VMEM((2, 2, bs, bs), F32),
            pltpu.VMEM((ITERS, 2, cols, bs), F32),
            pltpu.VMEM((ITERS, 2, 2, cols, bs), F32),
            pltpu.VMEM((ITERS, 2, 2, cols, bs), F32),
            dma((6,)),
            dma((2, 2)),
            dma((2, 2)),
            dma((ITERS, 2)),
            dma((ITERS, 2)),
            dma((ITERS, 2)),
            dma((ITERS, 2)),
            dma((ITERS, half - 1)),
            dma((ITERS, half - 1)),
            dma((ITERS, nc - 1)),
            dma((ITERS, nc - 1)),
            dma((ITERS,)),
            dma((ITERS,)),
        ],
        compiler_params=pltpu.CompilerParams(
            collective_id=0, has_side_effects=True, vmem_limit_bytes=56 * 1024 * 1024
        ),
    )(
        loads.reshape(cols * nb, bs), diag[0], offs[0], oidx[0].T, couple[0],
        basis.reshape(k * nb, bs), cblk[0], cidx[0],
    )
    return sol.transpose(1, 0, 2)[None], res.transpose(1, 0, 2)[None]


def solution(mesh):
    lead = ("sub", "coarse")
    in_specs = (
        P(lead, None, None, None),
        P(lead, None, None, None),
        P(lead, None, None, None, None),
        P(lead, None, None),
        P(lead, None, None, None),
        P(lead, None, None, None),
        P(lead, None, None, None),
        P(lead, None),
    )
    out_specs = (P(lead, None, None, None), P(lead, None, None, None))
    return jax.shard_map(
        functools.partial(per_device, mesh.shape["sub"], mesh.shape["coarse"]),
        mesh=mesh, in_specs=in_specs, out_specs=out_specs, check_vma=False,
    )
```

```python
import functools

import jax
import jax.numpy as jnp
from jax import lax
from jax.experimental import pallas as pl
from jax.experimental.pallas import tpu as pltpu
from jax.sharding import PartitionSpec as P

ORDER = 5
ITERS = 2
PARTS = 2
THETA = 5.0
DELTA = 4.0
F32 = jnp.float32
BF16 = jnp.bfloat16
MESH = pl.DeviceIdType.MESH


def cheb_coefs():
    sigma = THETA / DELTA
    rho = 1.0 / sigma
    out = []
    for _ in range(ORDER - 1):
        nxt = 1.0 / (2.0 * sigma - rho)
        out.append((nxt * rho, 2.0 * nxt / DELTA))
        rho = nxt
    return out


def halves(v):
    hi = v.astype(BF16)
    lo = (v - hi.astype(F32)).astype(BF16)
    return hi, lo


def dot_nt(x, w):
    return lax.dot_general(x, w, (((1,), (1,)), ((), ())), preferred_element_type=F32)


def dot_nn(x, w):
    return lax.dot_general(x, w, (((1,), (0,)), ((), ())), preferred_element_type=F32)


def kernel(
    ns, nc, nb, cols, bs, ncb,
    loads, diag, offs, oidx, couple, basis, cblk, cidx,
    sol, res,
    f_loads, f_diag, f_offs, f_couple, f_basis, f_cblk,
    w, wc, wt, bw, cw,
    r, d, z, ua, ub, ur,
    gath0, gath1, op_in, r_in, e_in, e_out,
    lsem, op_s, op_r, rh_s, rh_r, e_s, e_r, g1_s, g1_r, g2_s, g2_r, g3_s, g3_r,
):
    me_s = lax.axis_index("sub")
    me_x = lax.axis_index("coarse")
    core = lax.rem(me_s, 2)
    h = me_s // 2
    half = ns // 2
    partner = me_s + 1 - 2 * core
    has_l = me_s > 0
    has_r = me_s < ns - 1
    nb2 = nb // 2
    left, right = nb, nb + 1

    ld = [
        pltpu.make_async_copy(loads, f_loads, lsem.at[0]),
        pltpu.make_async_copy(basis, f_basis, lsem.at[1]),
        pltpu.make_async_copy(couple, f_couple, lsem.at[2]),
        pltpu.make_async_copy(diag, f_diag, lsem.at[3]),
        pltpu.make_async_copy(offs, f_offs, lsem.at[4]),
        pltpu.make_async_copy(cblk, f_cblk, lsem.at[5]),
    ]
    for c in ld:
        c.start()

    def remote(src, dst, ss, rs, s, x):
        return pltpu.make_async_remote_copy(
            src_ref=src, dst_ref=dst, send_sem=ss, recv_sem=rs,
            device_id={"sub": s, "coarse": x}, device_id_type=MESH,
        )

    barrier = pltpu.get_barrier_semaphore()

    def greet(s, x):
        pl.semaphore_signal(
            barrier, inc=1, device_id={"sub": s, "coarse": x}, device_id_type=MESH
        )

    for k in range(1, half):
        greet(core + 2 * lax.rem(h + k, half), me_x)
    for k in range(1, nc):
        greet(me_s, lax.rem(me_x + k, nc))

    @pl.when(has_l)
    def _():
        greet(me_s - 1, me_x)

    @pl.when(has_r)
    def _():
        greet(me_s + 1, me_x)

    def put(ref, b, v):
        hi, lo = halves(v)
        ref[b, 0:cols, :] = hi
        ref[b, cols : 2 * cols, :] = lo

    def fold(o):
        return (o[:cols, :bs] + o[:cols, bs:]) + (o[cols:, :bs] + o[cols:, bs:])

    ld[0].wait()

    def init_r(b, carry):
        v = f_loads[pl.ds(b, cols, stride=nb), :]
        r[b] = v
        put(ur, b, v)
        return carry

    lax.fori_loop(0, nb, init_r, 0)
    ld[1].wait()

    def init_bw(t, carry):
        for p in range(2):
            v = f_basis[pl.ds(2 * t + p, bs, stride=nb), :]
            hi, lo = halves(v)
            bw[t, 0:bs, p * bs : (p + 1) * bs] = hi
            bw[t, bs : 2 * bs, p * bs : (p + 1) * bs] = lo
        return carry

    lax.fori_loop(0, nb2, init_bw, 0)

    pl.semaphore_wait(barrier, half - 1 + nc - 1 + has_l.astype(jnp.int32) + has_r.astype(jnp.int32))

    def op_copies(to_left):
        b = 0 if to_left else nb - 1
        side = 1 if to_left else 0
        s = me_s - 1 if to_left else me_s + 1
        return [
            remote(f_diag.at[b], op_in.at[side, 0], op_s.at[side, 0], op_r.at[side, 0], s, me_x),
            remote(
                f_couple.at[0 if to_left else 1], op_in.at[side, 1],
                op_s.at[side, 1], op_r.at[side, 1], s, me_x,
            ),
        ]

    def r_copy(it, to_left):
        b = 0 if to_left else nb - 1
        side = 1 if to_left else 0
        s = me_s - 1 if to_left else me_s + 1
        return [remote(r.at[b], r_in.at[it, side], rh_s.at[it, side], rh_r.at[it, side], s, me_x)]

    def e_copy(it, to_left):
        side = 1 if to_left else 0
        s = me_s - 1 if to_left else me_s + 1
        return [
            remote(
                e_out.at[it, side], e_in.at[it, side], e_s.at[it, side], e_r.at[it, side], s, me_x
            )
        ]

    def start_both(make):
        @pl.when(has_l)
        def _():
            for c in make(True):
                c.start()

        @pl.when(has_r)
        def _():
            for c in make(False):
                c.start()

    def wait_both(make):
        @pl.when(has_l)
        def _():
            for c in make(True):
                c.wait_send()
            for c in make(False):
                c.wait_recv()

        @pl.when(has_r)
        def _():
            for c in make(False):
                c.wait_send()
            for c in make(True):
                c.wait_recv()

    for side, has in ((0, has_l), (1, has_r)):

        @pl.when(jnp.logical_not(has))
        def _():
            op_in[side] = jnp.zeros_like(op_in[side])
            for it in range(ITERS):
                r_in[it, side] = jnp.zeros_like(r_in[it, side])
                e_in[it, side] = jnp.zeros_like(e_in[it, side])

    own = me_x * half + h
    gath = (gath0, gath1)

    def part(p):
        return pl.ds(p * (cols // PARTS), cols // PARTS)

    def g1(it, p):
        return [
            remote(
                gath[it].at[core, own, part(p)], gath[it].at[core, own, part(p)],
                g1_s.at[it * PARTS + p, k - 1], g1_r.at[it * PARTS + p, k - 1],
                core + 2 * lax.rem(h + k, half), me_x,
            )
            for k in range(1, half)
        ]

    def g2(it, p):
        span = pl.ds(me_x * half, half)
        return [
            remote(
                gath[it].at[core, span, part(p)], gath[it].at[core, span, part(p)],
                g2_s.at[it * PARTS + p, k - 1], g2_r.at[it * PARTS + p, k - 1],
                me_s, lax.rem(me_x + k, nc),
            )
            for k in range(1, nc)
        ]

    def g3(it, p):
        return [
            remote(
                gath[it].at[core, :, part(p)], gath[it].at[core, :, part(p)],
                g3_s.at[it * PARTS + p], g3_r.at[it * PARTS + p], partner, me_x,
            )
        ]

    def start(copies):
        for c in copies:
            c.start()

    def wait(copies):
        for c in copies:
            c.wait()

    def coeffs(it):
        def body(q, acc):
            for p in range(4):
                t = 4 * q + p
                x = jnp.concatenate([ur[2 * t], ur[2 * t + 1]], axis=1)
                acc = acc + dot_nt(x, bw[t])
            return acc

        acc = lax.fori_loop(0, nb2 // 4, body, jnp.zeros((2 * cols, 2 * bs), F32))
        gath[it][core, own] = fold(acc)

    def row(u, b):
        x = jnp.concatenate([u[b], u[oidx[0, b]], u[oidx[1, b]]], axis=1)
        return fold(dot_nn(x, w[b]))

    GROUP = 15
    BATCH = 5

    def middle(u, emit):
        def body(q, carry):
            for first in range(0, GROUP, BATCH):
                rows = [1 + q * GROUP + first + p for p in range(BATCH)]
                emit(rows, [row(u, b) for b in rows])
            return carry

        if GROUP == nb - 2:
            body(0, 0)
        else:
            lax.fori_loop(0, (nb - 2) // GROUP, body, 0)

    def first_last(u):
        y0 = row(u, 0) + fold(dot_nn(u[left], wc[0]))
        y1 = row(u, nb - 1) + fold(dot_nn(u[right], wc[1]))
        return y0, y1

    def outer(u):
        yl = fold(dot_nn(jnp.concatenate([u[left], u[0]], axis=1), wt[0]))
        yr = fold(dot_nn(jnp.concatenate([u[right], u[nb - 1]], axis=1), wt[1]))
        return yl, yr

    coefs = cheb_coefs()

    def emit_step(k, unew):
        ca, cc = coefs[k]

        def emit(rows, ys):
            out = []
            for b, y in zip(rows, ys):
                rv = r[b]
                if k == 0:
                    dv = rv * (1.0 / THETA)
                    zv = dv
                    y = y * (1.0 / THETA)
                else:
                    dv = d[b]
                    zv = z[b]
                dv = ca * dv + cc * (rv - y)
                out.append((dv, zv + dv))
            for b, (dv, zv) in zip(rows, out):
                if k + 2 < ORDER:
                    d[b] = dv
                    put(unew, b, zv)
                z[b] = zv

        return emit

    def ends_step(k, u, unew):
        yl, yr = outer(u)
        y0, y1 = first_last(u)
        emit_step(k, unew)([0, nb - 1, left, right], [y0, y1, yl, yr])

    def iteration(it):
        last = it + 1 == ITERS
        middle(ur, emit_step(0, ua))
        wait_both(functools.partial(r_copy, it))
        for side, b in ((0, left), (1, right)):
            v = r_in[it, side]
            r[b] = v
            put(ur, b, v)
        ends_step(0, ur, ua)
        wait(g1(it, 0))
        start(g2(it, 0))
        middle(ua, emit_step(1, ub))
        ends_step(1, ua, ub)
        wait(g1(it, 1))
        start(g2(it, 1))
        middle(ub, emit_step(2, ua))
        ends_step(2, ub, ua)
        wait(g2(it, 0))
        start(g3(it, 0))
        ends_step(3, ua, ub)
        middle(ua, emit_step(3, ub))
        wait(g2(it, 1))
        start(g3(it, 1))
        wait(g3(it, 0))
        wait(g3(it, 1))

        xs = []
        for j in range(ncb):
            g = cidx[j]
            s = g // nc
            x = lax.rem(g, nc)
            hi, lo = halves(gath[it][lax.rem(s, 2), x * half + s // 2])
            xs.append(jnp.concatenate([hi, lo], axis=0))
        csol = fold(dot_nt(jnp.concatenate(xs, axis=1), cw[...]))
        hi, lo = halves(csol)
        cx = jnp.concatenate([hi, lo], axis=0)
        cx = jnp.concatenate([cx, cx], axis=1)

        def spread(t):
            o = dot_nn(cx, bw[t])
            o = o[:cols] + o[cols:]
            return o[:, :bs], o[:, bs:]

        def keep(b, v):
            sol[b] = v if it == 0 else sol[b] + v
            put(ub, b, v)

        a0, a1 = spread(0)
        b0, b1 = spread(nb2 - 1)
        edge_l = z[0] + a0
        edge_r = z[nb - 1] + b1
        e_out[it, 1, 0] = z[left]
        e_out[it, 1, 1] = edge_l
        e_out[it, 0, 0] = z[right]
        e_out[it, 0, 1] = edge_r
        start_both(functools.partial(e_copy, it))
        keep(1, z[1] + a1)
        keep(nb - 2, z[nb - 2] + b0)

        def spread_body(q, carry):
            for p in range(2):
                t = 1 + 2 * q + p
                v0, v1 = spread(t)
                keep(2 * t, z[2 * t] + v0)
                keep(2 * t + 1, z[2 * t + 1] + v1)
            return carry

        lax.fori_loop(0, (nb2 - 2) // 2, spread_body, 0)
        wait_both(functools.partial(e_copy, it))
        keep(0, edge_l + e_in[it, 0, 0])
        keep(nb - 1, edge_r + e_in[it, 1, 0])
        put(ub, left, e_in[it, 0, 1] + z[left])
        put(ub, right, e_in[it, 1, 1] + z[right])

        def emit_res(rows, ys):
            vals = [r[b] - y for b, y in zip(rows, ys)]
            for b, v in zip(rows, vals):
                if last:
                    res[b] = v
                else:
                    r[b] = v
                    put(ur, b, v)

        emit_res([0, nb - 1], list(first_last(ub)))
        if not last:
            start_both(functools.partial(r_copy, it + 1))
        middle(ub, emit_res)
        if not last:
            coeffs(it + 1)
            start(g1(it + 1, 0))
            start(g1(it + 1, 1))

    start_both(functools.partial(r_copy, 0))
    coeffs(0)
    start(g1(0, 0))
    start(g1(0, 1))
    ld[2].wait()
    ld[3].wait()
    start_both(op_copies)
    ld[4].wait()

    def init_w(b, carry):
        for j, v in enumerate((f_diag[b], f_offs[b, 0], f_offs[b, 1])):
            hi, lo = halves(v.T)
            w[b, j * bs : (j + 1) * bs, 0:bs] = hi
            w[b, j * bs : (j + 1) * bs, bs : 2 * bs] = lo
        return carry

    lax.fori_loop(0, nb, init_w, 0)
    for j in range(2):
        hi, lo = halves(f_couple[j].T)
        wc[j, :, 0:bs] = hi
        wc[j, :, bs : 2 * bs] = lo
    ld[5].wait()
    for j in range(ncb):
        hi, lo = halves(f_cblk[j])
        cw[0:bs, j * bs : (j + 1) * bs] = hi
        cw[bs : 2 * bs, j * bs : (j + 1) * bs] = lo
    wait_both(op_copies)
    for side in range(2):
        for j in range(2):
            hi, lo = halves(op_in[side, j].T)
            wt[side, j * bs : (j + 1) * bs, 0:bs] = hi
            wt[side, j * bs : (j + 1) * bs, bs : 2 * bs] = lo

    for it in range(ITERS):
        iteration(it)


def per_device(ns, nc, loads, diag, offs, oidx, couple, basis, cblk, cidx):
    _, cols, nb, bs = loads.shape
    k = basis.shape[1]
    ncb = cblk.shape[1]
    half = ns // 2
    anyspace = pl.BlockSpec(memory_space=pl.ANY)
    smem = pl.BlockSpec(memory_space=pltpu.SMEM)
    vmem = pl.BlockSpec(memory_space=pltpu.VMEM)
    field = (nb + 2, cols, bs)
    ufield = (nb + 2, 2 * cols, bs)
    dma = pltpu.SemaphoreType.DMA
    out = jax.ShapeDtypeStruct((nb, cols, bs), F32)
    sol, res = pl.pallas_call(
        functools.partial(kernel, ns, nc, nb, cols, bs, ncb),
        out_shape=(out, out),
        in_specs=[anyspace, anyspace, anyspace, smem, anyspace, anyspace, anyspace, smem],
        out_specs=(vmem, vmem),
        scratch_shapes=[
            pltpu.VMEM((cols * nb, bs), F32),
            pltpu.VMEM((nb, bs, bs), F32),
            pltpu.VMEM((nb, 2, bs, bs), F32),
            pltpu.VMEM((2, bs, bs), F32),
            pltpu.VMEM((k * nb, bs), F32),
            pltpu.VMEM((ncb, bs, bs), F32),
            pltpu.VMEM((nb, 3 * bs, 2 * bs), BF16),
            pltpu.VMEM((2, bs, 2 * bs), BF16),
            pltpu.VMEM((2, 2 * bs, 2 * bs), BF16),
            pltpu.VMEM((nb // 2, 2 * bs, 2 * bs), BF16),
            pltpu.VMEM((2 * bs, ncb * bs), BF16),
            pltpu.VMEM(field, F32),
            pltpu.VMEM(field, F32),
            pltpu.VMEM(field, F32),
            pltpu.VMEM(ufield, BF16),
            pltpu.VMEM(ufield, BF16),
            pltpu.VMEM(ufield, BF16),
            pltpu.VMEM((2, nc * half, cols, bs), F32),
            pltpu.VMEM((2, nc * half, cols, bs), F32),
            pltpu.VMEM((2, 2, bs, bs), F32),
            pltpu.VMEM((ITERS, 2, cols, bs), F32),
            pltpu.VMEM((ITERS, 2, 2, cols, bs), F32),
            pltpu.VMEM((ITERS, 2, 2, cols, bs), F32),
            dma((6,)),
            dma((2, 2)),
            dma((2, 2)),
            dma((ITERS, 2)),
            dma((ITERS, 2)),
            dma((ITERS, 2)),
            dma((ITERS, 2)),
            dma((ITERS * PARTS, half - 1)),
            dma((ITERS * PARTS, half - 1)),
            dma((ITERS * PARTS, nc - 1)),
            dma((ITERS * PARTS, nc - 1)),
            dma((ITERS * PARTS,)),
            dma((ITERS * PARTS,)),
        ],
        compiler_params=pltpu.CompilerParams(
            collective_id=0, has_side_effects=True, vmem_limit_bytes=56 * 1024 * 1024
        ),
    )(
        loads.reshape(cols * nb, bs), diag[0], offs[0], oidx[0].T, couple[0],
        basis.reshape(k * nb, bs), cblk[0], cidx[0],
    )
    return sol.transpose(1, 0, 2)[None], res.transpose(1, 0, 2)[None]


def solution(mesh):
    lead = ("sub", "coarse")
    in_specs = (
        P(lead, None, None, None),
        P(lead, None, None, None),
        P(lead, None, None, None, None),
        P(lead, None, None),
        P(lead, None, None, None),
        P(lead, None, None, None),
        P(lead, None, None, None),
        P(lead, None),
    )
    out_specs = (P(lead, None, None, None), P(lead, None, None, None))
    return jax.shard_map(
        functools.partial(per_device, mesh.shape["sub"], mesh.shape["coarse"]),
        mesh=mesh, in_specs=in_specs, out_specs=out_specs, check_vma=False,
    )
```

```python
import functools

import jax
import jax.numpy as jnp
from jax import lax
from jax.experimental import pallas as pl
from jax.experimental.pallas import tpu as pltpu
from jax.sharding import PartitionSpec as P

ORDER = 5
ITERS = 2
THETA = 5.0
DELTA = 4.0
F32 = jnp.float32
BF16 = jnp.bfloat16
MESH = pl.DeviceIdType.MESH


def cheb_coefs():
    sigma = THETA / DELTA
    rho = 1.0 / sigma
    out = []
    for _ in range(ORDER - 1):
        nxt = 1.0 / (2.0 * sigma - rho)
        out.append((nxt * rho, 2.0 * nxt / DELTA))
        rho = nxt
    return out


def halves(v):
    hi = v.astype(BF16)
    lo = (v - hi.astype(F32)).astype(BF16)
    return hi, lo


def dot_nt(x, w):
    return lax.dot_general(x, w, (((1,), (1,)), ((), ())), preferred_element_type=F32)


def dot_nn(x, w):
    return lax.dot_general(x, w, (((1,), (0,)), ((), ())), preferred_element_type=F32)


def kernel(
    ns, nc, nb, cols, bs, ncb,
    loads, diag, offs, oidx, couple, basis, cblk, cidx,
    sol, res,
    f_loads, f_diag, f_offs, f_couple, f_basis, f_cblk,
    w, wc, wt, bw, cw,
    r, d, z, ua, ub, ur,
    gath0, gath1, op_in, r_in, e_in, e_out,
    lsem, op_s, op_r, rh_s, rh_r, e_s, e_r, g1_s, g1_r, g2_s, g2_r, g3_s, g3_r,
):
    me_s = lax.axis_index("sub")
    me_x = lax.axis_index("coarse")
    core = lax.rem(me_s, 2)
    h = me_s // 2
    half = ns // 2
    partner = me_s + 1 - 2 * core
    has_l = me_s > 0
    has_r = me_s < ns - 1
    nb2 = nb // 2
    left, right = nb, nb + 1

    ld = [
        pltpu.make_async_copy(loads, f_loads, lsem.at[0]),
        pltpu.make_async_copy(basis, f_basis, lsem.at[1]),
        pltpu.make_async_copy(couple, f_couple, lsem.at[2]),
        pltpu.make_async_copy(diag, f_diag, lsem.at[3]),
        pltpu.make_async_copy(offs, f_offs, lsem.at[4]),
        pltpu.make_async_copy(cblk, f_cblk, lsem.at[5]),
    ]
    for c in ld:
        c.start()

    def remote(src, dst, ss, rs, s, x):
        return pltpu.make_async_remote_copy(
            src_ref=src, dst_ref=dst, send_sem=ss, recv_sem=rs,
            device_id={"sub": s, "coarse": x}, device_id_type=MESH,
        )

    barrier = pltpu.get_barrier_semaphore()

    def greet(s, x):
        pl.semaphore_signal(
            barrier, inc=1, device_id={"sub": s, "coarse": x}, device_id_type=MESH
        )

    for k in range(1, half):
        greet(core + 2 * lax.rem(h + k, half), me_x)
    for k in range(1, nc):
        greet(me_s, lax.rem(me_x + k, nc))

    @pl.when(has_l)
    def _():
        greet(me_s - 1, me_x)

    @pl.when(has_r)
    def _():
        greet(me_s + 1, me_x)

    def put(ref, b, v):
        hi, lo = halves(v)
        ref[b, 0:cols, :] = hi
        ref[b, cols : 2 * cols, :] = lo

    def fold(o):
        return (o[:cols, :bs] + o[:cols, bs:]) + (o[cols:, :bs] + o[cols:, bs:])

    ld[0].wait()

    def init_r(b, carry):
        v = f_loads[pl.ds(b, cols, stride=nb), :]
        r[b] = v
        put(ur, b, v)
        return carry

    lax.fori_loop(0, nb, init_r, 0)
    pl.semaphore_wait(barrier, half - 1 + nc - 1 + has_l.astype(jnp.int32) + has_r.astype(jnp.int32))

    def op_copies(to_left):
        b = 0 if to_left else nb - 1
        side = 1 if to_left else 0
        s = me_s - 1 if to_left else me_s + 1
        return [
            remote(diag.at[b], op_in.at[side, 0], op_s.at[side, 0], op_r.at[side, 0], s, me_x),
            remote(
                couple.at[0 if to_left else 1], op_in.at[side, 1],
                op_s.at[side, 1], op_r.at[side, 1], s, me_x,
            ),
        ]

    def r_copy(it, to_left):
        b = 0 if to_left else nb - 1
        side = 1 if to_left else 0
        s = me_s - 1 if to_left else me_s + 1
        return [remote(r.at[b], r_in.at[it, side], rh_s.at[it, side], rh_r.at[it, side], s, me_x)]

    def e_copy(it, to_left):
        side = 1 if to_left else 0
        s = me_s - 1 if to_left else me_s + 1
        return [
            remote(
                e_out.at[it, side], e_in.at[it, side], e_s.at[it, side], e_r.at[it, side], s, me_x
            )
        ]

    def start_both(make):
        @pl.when(has_l)
        def _():
            for c in make(True):
                c.start()

        @pl.when(has_r)
        def _():
            for c in make(False):
                c.start()

    def wait_both(make):
        @pl.when(has_l)
        def _():
            for c in make(True):
                c.wait_send()
            for c in make(False):
                c.wait_recv()

        @pl.when(has_r)
        def _():
            for c in make(False):
                c.wait_send()
            for c in make(True):
                c.wait_recv()

    for side, has in ((0, has_l), (1, has_r)):

        @pl.when(jnp.logical_not(has))
        def _():
            op_in[side] = jnp.zeros_like(op_in[side])
            for it in range(ITERS):
                r_in[it, side] = jnp.zeros_like(r_in[it, side])
                e_in[it, side] = jnp.zeros_like(e_in[it, side])

    start_both(op_copies)
    ld[1].wait()

    def init_bw(t, carry):
        for p in range(2):
            v = f_basis[pl.ds(2 * t + p, bs, stride=nb), :]
            hi, lo = halves(v)
            bw[t, 0:bs, p * bs : (p + 1) * bs] = hi
            bw[t, bs : 2 * bs, p * bs : (p + 1) * bs] = lo
        return carry

    lax.fori_loop(0, nb2, init_bw, 0)

    own = me_x * half + h
    gath = (gath0, gath1)

    def g1(it):
        return [
            remote(
                gath[it].at[core, own], gath[it].at[core, own],
                g1_s.at[it, k - 1], g1_r.at[it, k - 1],
                core + 2 * lax.rem(h + k, half), me_x,
            )
            for k in range(1, half)
        ]

    def g2(it):
        span = pl.ds(me_x * half, half)
        return [
            remote(
                gath[it].at[core, span], gath[it].at[core, span],
                g2_s.at[it, k - 1], g2_r.at[it, k - 1],
                me_s, lax.rem(me_x + k, nc),
            )
            for k in range(1, nc)
        ]

    def g3(it):
        return [
            remote(
                gath[it].at[core], gath[it].at[core], g3_s.at[it], g3_r.at[it], partner, me_x
            )
        ]

    def start(copies):
        for c in copies:
            c.start()

    def wait(copies):
        for c in copies:
            c.wait()

    def coeffs(it):
        def body(q, acc):
            for p in range(4):
                t = 4 * q + p
                x = jnp.concatenate([ur[2 * t], ur[2 * t + 1]], axis=1)
                acc = acc + dot_nt(x, bw[t])
            return acc

        acc = lax.fori_loop(0, nb2 // 4, body, jnp.zeros((2 * cols, 2 * bs), F32))
        gath[it][core, own] = fold(acc)

    def row(u, b):
        x = jnp.concatenate([u[b], u[oidx[0, b]], u[oidx[1, b]]], axis=1)
        return fold(dot_nn(x, w[b]))

    GROUP = 15
    BATCH = 5

    def middle(u, emit):
        def body(q, carry):
            for first in range(0, GROUP, BATCH):
                rows = [1 + q * GROUP + first + p for p in range(BATCH)]
                emit(rows, [row(u, b) for b in rows])
            return carry

        if GROUP == nb - 2:
            body(0, 0)
        else:
            lax.fori_loop(0, (nb - 2) // GROUP, body, 0)

    def first_last(u):
        y0 = row(u, 0) + fold(dot_nn(u[left], wc[0]))
        y1 = row(u, nb - 1) + fold(dot_nn(u[right], wc[1]))
        return y0, y1

    def outer(u):
        yl = fold(dot_nn(jnp.concatenate([u[left], u[0]], axis=1), wt[0]))
        yr = fold(dot_nn(jnp.concatenate([u[right], u[nb - 1]], axis=1), wt[1]))
        return yl, yr

    coefs = cheb_coefs()

    def emit_step(k, unew):
        ca, cc = coefs[k]

        def emit(rows, ys):
            out = []
            for b, y in zip(rows, ys):
                rv = r[b]
                if k == 0:
                    dv = rv * (1.0 / THETA)
                    zv = dv
                    y = y * (1.0 / THETA)
                else:
                    dv = d[b]
                    zv = z[b]
                dv = ca * dv + cc * (rv - y)
                out.append((dv, zv + dv))
            for b, (dv, zv) in zip(rows, out):
                if k + 2 < ORDER:
                    d[b] = dv
                    put(unew, b, zv)
                z[b] = zv

        return emit

    def ends_step(k, u, unew):
        yl, yr = outer(u)
        y0, y1 = first_last(u)
        emit_step(k, unew)([0, nb - 1, left, right], [y0, y1, yl, yr])

    def outer_operator():
        wait_both(op_copies)
        for side in range(2):
            for j in range(2):
                hi, lo = halves(op_in[side, j].T)
                wt[side, j * bs : (j + 1) * bs, 0:bs] = hi
                wt[side, j * bs : (j + 1) * bs, bs : 2 * bs] = lo

    def iteration(it):
        last = it + 1 == ITERS
        middle(ur, emit_step(0, ua))
        if it == 0:
            outer_operator()
        wait_both(functools.partial(r_copy, it))
        for side, b in ((0, left), (1, right)):
            v = r_in[it, side]
            r[b] = v
            put(ur, b, v)
        ends_step(0, ur, ua)
        wait(g1(it))
        start(g2(it))
        middle(ua, emit_step(1, ub))
        ends_step(1, ua, ub)
        middle(ub, emit_step(2, ua))
        ends_step(2, ub, ua)
        wait(g2(it))
        start(g3(it))
        ends_step(3, ua, ub)
        middle(ua, emit_step(3, ub))
        wait(g3(it))

        xs = []
        for j in range(ncb):
            g = cidx[j]
            s = g // nc
            x = lax.rem(g, nc)
            hi, lo = halves(gath[it][lax.rem(s, 2), x * half + s // 2])
            xs.append(jnp.concatenate([hi, lo], axis=0))
        csol = fold(dot_nt(jnp.concatenate(xs, axis=1), cw[...]))
        hi, lo = halves(csol)
        cx = jnp.concatenate([hi, lo], axis=0)
        cx = jnp.concatenate([cx, cx], axis=1)

        def spread(t):
            o = dot_nn(cx, bw[t])
            o = o[:cols] + o[cols:]
            return o[:, :bs], o[:, bs:]

        def keep(b, v):
            sol[b] = v if it == 0 else sol[b] + v
            put(ub, b, v)

        a0, a1 = spread(0)
        b0, b1 = spread(nb2 - 1)
        edge_l = z[0] + a0
        edge_r = z[nb - 1] + b1
        e_out[it, 1, 0] = z[left]
        e_out[it, 1, 1] = edge_l
        e_out[it, 0, 0] = z[right]
        e_out[it, 0, 1] = edge_r
        start_both(functools.partial(e_copy, it))
        keep(1, z[1] + a1)
        keep(nb - 2, z[nb - 2] + b0)

        def spread_body(q, carry):
            for p in range(2):
                t = 1 + 2 * q + p
                v0, v1 = spread(t)
                keep(2 * t, z[2 * t] + v0)
                keep(2 * t + 1, z[2 * t + 1] + v1)
            return carry

        lax.fori_loop(0, (nb2 - 2) // 2, spread_body, 0)
        wait_both(functools.partial(e_copy, it))
        keep(0, edge_l + e_in[it, 0, 0])
        keep(nb - 1, edge_r + e_in[it, 1, 0])
        put(ub, left, e_in[it, 0, 1] + z[left])
        put(ub, right, e_in[it, 1, 1] + z[right])

        def emit_res(rows, ys):
            vals = [r[b] - y for b, y in zip(rows, ys)]
            for b, v in zip(rows, vals):
                if last:
                    res[b] = v
                else:
                    r[b] = v
                    put(ur, b, v)

        emit_res([0, nb - 1], list(first_last(ub)))
        if not last:
            start_both(functools.partial(r_copy, it + 1))
        middle(ub, emit_res)
        if not last:
            coeffs(it + 1)
            start(g1(it + 1))

    start_both(functools.partial(r_copy, 0))
    coeffs(0)
    start(g1(0))
    ld[2].wait()
    ld[3].wait()
    ld[4].wait()

    def init_w(b, carry):
        for j, v in enumerate((f_diag[b], f_offs[b, 0], f_offs[b, 1])):
            hi, lo = halves(v.T)
            w[b, j * bs : (j + 1) * bs, 0:bs] = hi
            w[b, j * bs : (j + 1) * bs, bs : 2 * bs] = lo
        return carry

    lax.fori_loop(0, nb, init_w, 0)
    for j in range(2):
        hi, lo = halves(f_couple[j].T)
        wc[j, :, 0:bs] = hi
        wc[j, :, bs : 2 * bs] = lo
    ld[5].wait()
    for j in range(ncb):
        hi, lo = halves(f_cblk[j])
        cw[0:bs, j * bs : (j + 1) * bs] = hi
        cw[bs : 2 * bs, j * bs : (j + 1) * bs] = lo
    for it in range(ITERS):
        iteration(it)


def per_device(ns, nc, loads, diag, offs, oidx, couple, basis, cblk, cidx):
    _, cols, nb, bs = loads.shape
    k = basis.shape[1]
    ncb = cblk.shape[1]
    half = ns // 2
    anyspace = pl.BlockSpec(memory_space=pl.ANY)
    smem = pl.BlockSpec(memory_space=pltpu.SMEM)
    vmem = pl.BlockSpec(memory_space=pltpu.VMEM)
    field = (nb + 2, cols, bs)
    ufield = (nb + 2, 2 * cols, bs)
    dma = pltpu.SemaphoreType.DMA
    out = jax.ShapeDtypeStruct((nb, cols, bs), F32)
    sol, res = pl.pallas_call(
        functools.partial(kernel, ns, nc, nb, cols, bs, ncb),
        out_shape=(out, out),
        in_specs=[anyspace, anyspace, anyspace, smem, anyspace, anyspace, anyspace, smem],
        out_specs=(vmem, vmem),
        scratch_shapes=[
            pltpu.VMEM((cols * nb, bs), F32),
            pltpu.VMEM((nb, bs, bs), F32),
            pltpu.VMEM((nb, 2, bs, bs), F32),
            pltpu.VMEM((2, bs, bs), F32),
            pltpu.VMEM((k * nb, bs), F32),
            pltpu.VMEM((ncb, bs, bs), F32),
            pltpu.VMEM((nb, 3 * bs, 2 * bs), BF16),
            pltpu.VMEM((2, bs, 2 * bs), BF16),
            pltpu.VMEM((2, 2 * bs, 2 * bs), BF16),
            pltpu.VMEM((nb // 2, 2 * bs, 2 * bs), BF16),
            pltpu.VMEM((2 * bs, ncb * bs), BF16),
            pltpu.VMEM(field, F32),
            pltpu.VMEM(field, F32),
            pltpu.VMEM(field, F32),
            pltpu.VMEM(ufield, BF16),
            pltpu.VMEM(ufield, BF16),
            pltpu.VMEM(ufield, BF16),
            pltpu.VMEM((2, nc * half, cols, bs), F32),
            pltpu.VMEM((2, nc * half, cols, bs), F32),
            pltpu.VMEM((2, 2, bs, bs), F32),
            pltpu.VMEM((ITERS, 2, cols, bs), F32),
            pltpu.VMEM((ITERS, 2, 2, cols, bs), F32),
            pltpu.VMEM((ITERS, 2, 2, cols, bs), F32),
            dma((6,)),
            dma((2, 2)),
            dma((2, 2)),
            dma((ITERS, 2)),
            dma((ITERS, 2)),
            dma((ITERS, 2)),
            dma((ITERS, 2)),
            dma((ITERS, half - 1)),
            dma((ITERS, half - 1)),
            dma((ITERS, nc - 1)),
            dma((ITERS, nc - 1)),
            dma((ITERS,)),
            dma((ITERS,)),
        ],
        compiler_params=pltpu.CompilerParams(
            collective_id=0, has_side_effects=True, vmem_limit_bytes=56 * 1024 * 1024
        ),
    )(
        loads.reshape(cols * nb, bs), diag[0], offs[0], oidx[0].T, couple[0],
        basis.reshape(k * nb, bs), cblk[0], cidx[0],
    )
    return sol.transpose(1, 0, 2)[None], res.transpose(1, 0, 2)[None]


def solution(mesh):
    lead = ("sub", "coarse")
    in_specs = (
        P(lead, None, None, None),
        P(lead, None, None, None),
        P(lead, None, None, None, None),
        P(lead, None, None),
        P(lead, None, None, None),
        P(lead, None, None, None),
        P(lead, None, None, None),
        P(lead, None),
    )
    out_specs = (P(lead, None, None, None), P(lead, None, None, None))
    return jax.shard_map(
        functools.partial(per_device, mesh.shape["sub"], mesh.shape["coarse"]),
        mesh=mesh, in_specs=in_specs, out_specs=out_specs, check_vma=False,
    )
```
